32 devices in a mesh: groups: 2 (over y), loop: 4 (over z), heads: 2 (over x), pair: 2 (over core).
Axes of the slice: x: 2, y: 2, z: 4, core: 2. Of those that a mesh axis runs over, the one named last changes fastest.
Arguments:
- queries: bfloat16 [5120, 2048], P(('groups', 'loop'), ('heads', 'pair')), parts along dimension 0, may hold values from -96 to 96
- suffix_kv: bfloat16 [5120, 2, 256], P(('groups', 'loop'), 'heads'), parts along dimension 0, may hold values from -4 to 4
- prompt_kv: bfloat16 [2048, 2, 256], P(('groups', 'loop'), 'heads'), parts along dimension 0, may hold values from -4 to 4
- lengths: int32 [16], P('groups'), parts along dimension 0, may hold values from 128 to 320, as said below
Outputs:
- attended: bfloat16 [5120, 2048], P(('groups', 'loop'), ('heads', 'pair')), parts along dimension 0
The draws below stay inside these ranges and needn't reach their ends.
There are 2 independent parts, one for each index of `groups`. The reference program is written for one: setup_inputs(seed, part) draws one part's arguments, and reference() takes and returns one part's arrays. A program takes and returns all parts, laid end to end along the dimension named above; each array names one. Nothing has to cross between parts.
Inputs may be any that keep to these rules, and one draw needn't show every extreme that they name: Each agent's suffix has 128 to 320 tokens, and agents d * 2 to d * 2 + 1 belong to loop index d, so their lengths add up to at most 640 slots.
All inputs are finite; a program needn't handle non-finite values.
Results may differ from the reference program's by a relative error of at most 0.0065.
Values may be sent and summed in bfloat16 or wider, within the bound.
A program may use at most 64 MiB of HBM per device.

```python
import math
import jax
import jax.numpy as jnp
from jax import lax

HD = 128
QPK = 8
AG_DEV = 2
MINLEN = 128
MAXLEN = 320
KVH = 2
QH = 16
ROWS = 640
NTOT = 2560
AGENTS = 8
PROMPT = 1024
N_LOOP = 4


def prompt_keys(key):
    keys_drawn = jax.random.truncated_normal(jax.random.fold_in(key, 11), -4.0, 4.0, (PROMPT, KVH, HD), jnp.float32)
    return keys_drawn


def draw_prompt_kv(key, part):
    keys_drawn = prompt_keys(key)
    values_drawn = jax.random.truncated_normal(jax.random.fold_in(key, 12), -4.0, 4.0, (PROMPT, KVH, HD), jnp.float32)
    return jnp.concatenate([keys_drawn, values_drawn], axis=2).astype(jnp.bfloat16)


def draw_queries(key, part):
    drawn_queries = 2.5 * jax.random.truncated_normal(jax.random.fold_in(key, 13), -4.0, 4.0, (NTOT, QH * HD), jnp.float32)
    return drawn_queries.astype(jnp.bfloat16)


def draw_lengths(key, part):
    loop_count = NTOT // ROWS
    heavy_flag = jax.random.randint(jax.random.fold_in(key, 31), (loop_count,), 0, 4) == 0
    heavy_flag = heavy_flag.at[0].set(True).at[1].set(False)
    heavy_len = jax.random.randint(jax.random.fold_in(key, 32), (loop_count, AG_DEV), MAXLEN * 4 // 5, MAXLEN + 1)
    light_len = jax.random.randint(jax.random.fold_in(key, 33), (loop_count, AG_DEV), MINLEN, MAXLEN // 2 + 1)
    agent_lengths = jnp.where(heavy_flag[:, None], heavy_len, light_len)
    agent_lengths = agent_lengths.at[0, :].set(MAXLEN).at[1, 0].set(MINLEN)
    return agent_lengths.reshape(AGENTS).astype(jnp.int32)


def levels(key, dims, shards, low, top_value):
    def one(dim, parts):
        heights = jax.random.uniform(jax.random.fold_in(jax.random.fold_in(key, 6), dim), (parts,), jnp.float32, low / len(shards), top_value / len(shards))
        return jnp.repeat(jnp.exp(heights), dims[dim] // parts).reshape((-1,) + (1,) * (len(dims) - dim - 1))

    level = one(*shards[0])
    for cut in shards[1:]:
        level = level * one(*cut)
    return level


def scatter_about(stream_key, dims, width, limit, cuts=(), kind=jnp.bfloat16):
    values = jax.random.normal(stream_key, dims, jnp.float32) * width
    if len(cuts) > 0:
        values = levels(stream_key, dims, cuts, -0.22, 0.18) * values
    return jnp.clip(values, min=-limit, max=limit).astype(kind)


def setup_inputs(seed: int = 0, part: int = 0) -> dict:
    splits = jax.random.split(jax.random.key(seed), 5)
    own_keys = jax.random.split(jax.random.fold_in(splits[4], part), 5)
    return {
        "queries": draw_queries(jax.random.fold_in(jax.random.fold_in(splits[4], part), 71), part),
        "suffix_kv": scatter_about(own_keys[1], (NTOT, KVH, 2 * HD), 1.0, 4.0, ((0, 4), (1, 2))),
        "prompt_kv": draw_prompt_kv(jax.random.fold_in(jax.random.fold_in(splits[4], part), 71), part),
        "lengths": draw_lengths(jax.random.fold_in(jax.random.fold_in(splits[4], part), 71), part),
    }


def reference(queries, suffix_kv, prompt_kv, lengths):
    score_scale = 1.0 / math.sqrt(HD)
    positions = jnp.arange(ROWS, dtype=jnp.int32)

    def one_device(device):
        row_start = (device * ROWS).astype(jnp.int32)
        query_rows = lax.dynamic_slice_in_dim(queries, row_start, ROWS, 0)
        suffix_rows = lax.dynamic_slice_in_dim(suffix_kv, row_start, ROWS, 0)
        agent_lengths = lax.dynamic_slice_in_dim(lengths, (device * AG_DEV).astype(jnp.int32), AG_DEV, 0)
        agent_ends = jnp.cumsum(agent_lengths)
        agent_of = lax.optimization_barrier(jnp.sum((positions[:, None] >= agent_ends[None, :]).astype(jnp.int32), axis=1))
        live_rows = positions < agent_ends[-1]
        allowed = (agent_of[:, None] == agent_of[None, :]) & (positions[None, :] <= positions[:, None]) & live_rows[:, None]
        allowed = jnp.repeat(allowed, QPK, axis=0)
        live_rep = jnp.repeat(live_rows, QPK)

        def one_head(key_head):
            query_head = lax.dynamic_slice_in_dim(query_rows, (key_head * QPK * HD).astype(jnp.int32), QPK * HD, 1).reshape(ROWS * QPK, HD)
            prompt_head = lax.dynamic_index_in_dim(prompt_kv, key_head, 1, keepdims=False)
            suffix_head = lax.dynamic_index_in_dim(suffix_rows, key_head, 1, keepdims=False)
            prompt_scores = jnp.dot(query_head, prompt_head[:, :HD].T, preferred_element_type=jnp.float32) * score_scale
            suffix_scores = jnp.dot(query_head, suffix_head[:, :HD].T, preferred_element_type=jnp.float32) * score_scale
            suffix_scores = jnp.where(allowed, suffix_scores, -jnp.inf)
            row_best = jnp.maximum(lax.optimization_barrier(jnp.max(prompt_scores, axis=1)), lax.optimization_barrier(jnp.max(suffix_scores, axis=1)))
            prompt_weights = jnp.exp(prompt_scores - row_best[:, None])
            suffix_weights = jnp.where(allowed, jnp.exp(suffix_scores - row_best[:, None]), 0.0)
            row_total = lax.optimization_barrier(jnp.sum(prompt_weights, axis=1)) + lax.optimization_barrier(jnp.sum(suffix_weights, axis=1))
            weighted_sum = jnp.dot(prompt_weights.astype(jnp.bfloat16), prompt_head[:, HD:], preferred_element_type=jnp.float32)
            weighted_sum = weighted_sum + jnp.dot(suffix_weights.astype(jnp.bfloat16), suffix_head[:, HD:], preferred_element_type=jnp.float32)
            safe_total = jnp.where(live_rep, row_total, 1.0)
            result = jnp.where(live_rep[:, None], weighted_sum / safe_total[:, None], 0.0)
            return result.reshape(ROWS, QPK * HD)
        per_head = lax.map(one_head, jnp.arange(KVH, dtype=jnp.int32))
        return jnp.transpose(per_head, (1, 0, 2)).reshape(ROWS, KVH * QPK * HD).astype(jnp.bfloat16)
    outputs = lax.map(one_device, jnp.arange(N_LOOP, dtype=jnp.int32))
    return outputs.reshape(N_LOOP * ROWS, KVH * QPK * HD)
```

```python
import functools
import math

import jax
import jax.numpy as jnp
from jax import lax
from jax.experimental import pallas as pl
from jax.experimental.pallas import tpu as pltpu
from jax.sharding import PartitionSpec as P

HD = 128
AG_DEV = 2
MAXLEN = 320
TILE = 128
NEG = -1e30
MESH = pl.DeviceIdType.MESH


def ones_beside(values):
    return jnp.concatenate([values, jnp.ones_like(values)], axis=1)


def scores_of(q, keys):
    return lax.dot_general(q, keys, (((1,), (1,)), ((), ())), preferred_element_type=jnp.float32)


def kernel(n, factor, len_ref, q_ref, sfx_ref, prm_ref, out_ref, held, best, acc, send_sem, recv_sem, pass_sem, got_sem):
    rows, width = q_ref.shape
    heads = width // HD
    tiles = rows // TILE
    half = prm_ref.shape[0] // 2
    me = lax.axis_index("loop")
    core = lax.axis_index("pair")
    barrier = pltpu.get_barrier_semaphore()

    def each_other(do):
        for d in range(1, n):
            for other in (me - d, me + d):

                @pl.when((other >= 0) & (other < n))
                def _(other=other):
                    do(other)

    each_other(
        lambda other: pl.semaphore_signal(barrier, inc=1, device_id={"loop": other}, device_id_type=MESH)
    )
    pl.semaphore_signal(barrier, inc=1, device_id={"pair": 1 - core}, device_id_type=MESH)
    pl.semaphore_wait(barrier, n)

    def out_copy(other):
        return pltpu.make_async_remote_copy(
            src_ref=prm_ref.at[pl.ds(pl.multiple_of(core * half, half), half), :],
            dst_ref=held.at[me, core],
            send_sem=send_sem.at[other],
            recv_sem=recv_sem.at[me],
            device_id={"loop": other},
            device_id_type=MESH,
        )

    each_other(lambda other: out_copy(other).start())

    def source(k):
        both = jnp.minimum(me, n - 1 - me)
        near = (k + 1) // 2
        paired = jnp.where(k % 2 == 1, me - near, me + near)
        far = k - both
        lone = jnp.where(me > n - 1 - me, me - far, me + far)
        return jnp.where(k <= 2 * both, paired, lone)

    def arrived(src):
        pltpu.make_async_remote_copy(
            src_ref=held.at[src, core],
            dst_ref=held.at[src, core],
            send_sem=send_sem.at[src],
            recv_sem=recv_sem.at[src],
            device_id={"loop": src},
            device_id_type=MESH,
        ).wait_recv()

    def hand_over(src, which):
        return pltpu.make_async_remote_copy(
            src_ref=held.at[src, which],
            dst_ref=held.at[src, which],
            send_sem=pass_sem.at[src],
            recv_sem=got_sem.at[src],
            device_id={"pair": 1 - core},
            device_id_type=MESH,
        )

    first_end = len_ref[me * AG_DEV]
    live_end = first_end + len_ref[me * AG_DEV + 1]

    window_blocks = (MAXLEN + TILE - 2) // TILE + 1
    for t in range(tiles):
        at = t * TILE
        low = max(0, t + 1 - window_blocks) * TILE
        span = at + TILE - low
        row_at = at + lax.broadcasted_iota(jnp.int32, (TILE, span), 0)
        key_at = low + lax.broadcasted_iota(jnp.int32, (TILE, span), 1)
        begin = jnp.where(row_at >= first_end, first_end, 0)
        allowed = (key_at <= row_at) & (key_at >= begin)
        for h in range(heads):
            q = q_ref[pl.ds(at, TILE), pl.ds(h * HD, HD)]
            s_own = scores_of(q, prm_ref[:, :HD])
            s_sfx = scores_of(q, sfx_ref[pl.ds(low, span), :HD])
            s_sfx = jnp.where(allowed, s_sfx, NEG)
            top = jnp.maximum(
                jnp.max(s_own, axis=1, keepdims=True), jnp.max(s_sfx, axis=1, keepdims=True)
            )
            w_own = jnp.exp2((s_own - top) * factor).astype(jnp.bfloat16)
            w_sfx = jnp.exp2((s_sfx - top) * factor).astype(jnp.bfloat16)
            total = jnp.dot(w_own, ones_beside(prm_ref[:, HD:]), preferred_element_type=jnp.float32)
            total += jnp.dot(
                w_sfx, ones_beside(sfx_ref[pl.ds(low, span), HD:]), preferred_element_type=jnp.float32
            )
            best[pl.ds(at, TILE), pl.ds(h * HD, HD)] = jnp.broadcast_to(top, (TILE, HD))
            acc[pl.ds(at, TILE), pl.ds(h * 2 * HD, 2 * HD)] = total

    def fold(src, t, last):
        at = pl.multiple_of(t * TILE, TILE)
        block = held[src].reshape(2 * half, 2 * HD)
        keys, values = block[:, :HD], ones_beside(block[:, HD:])
        for h in range(heads):
            q = q_ref[pl.ds(at, TILE), pl.ds(h * HD, HD)]
            s = scores_of(q, keys)
            old = best[pl.ds(at, TILE), pl.ds(h * HD, HD)]
            top = jnp.maximum(old, jnp.max(s, axis=1, keepdims=True))
            shrink = jnp.exp2((old - top) * factor)
            w = jnp.exp2((s - jnp.concatenate([top] * (s.shape[1] // HD), axis=1)) * factor)
            new = jnp.dot(w.astype(jnp.bfloat16), values, preferred_element_type=jnp.float32)
            kept = acc[pl.ds(at, TILE), pl.ds(h * 2 * HD, 2 * HD)]
            total = kept * jnp.concatenate([shrink, shrink], axis=1) + new
            if last:
                row_at = at + lax.broadcasted_iota(jnp.int32, (TILE, HD), 0)
                result = jnp.where(row_at < live_end, total[:, :HD] / total[:, HD:], 0.0)
                out_ref[pl.ds(at, TILE), pl.ds(h * HD, HD)] = result.astype(out_ref.dtype)
            else:
                best[pl.ds(at, TILE), pl.ds(h * HD, HD)] = top
                acc[pl.ds(at, TILE), pl.ds(h * 2 * HD, 2 * HD)] = total

    def fold_all(src, last):
        hand_over(src, 1 - core).wait_recv()

        def one(t, carry):
            fold(src, t, last)
            return carry

        lax.fori_loop(0, tiles, one, 0)

    arrived(source(1))
    hand_over(source(1), core).start()

    def step(k, carry):
        following = source(k + 1)
        arrived(following)
        hand_over(following, core).start()
        fold_all(source(k), False)
        return carry

    lax.fori_loop(1, n - 1, step, 0)
    fold_all(source(n - 1), True)

    each_other(lambda other: out_copy(other).wait_send())
    each_other(lambda other: hand_over(other, core).wait_send())


def shards(queries, suffix_kv, prompt_kv, lengths):
    n = lax.axis_size("loop")
    rows, width = queries.shape
    heads = width // HD
    depth = prompt_kv.shape[0]
    factor = math.log2(math.e) / math.sqrt(HD)
    vmem = pl.BlockSpec(memory_space=pltpu.VMEM)
    return pl.pallas_call(
        functools.partial(kernel, n, factor),
        out_shape=jax.ShapeDtypeStruct((rows, width), jnp.bfloat16),
        in_specs=[pl.BlockSpec(memory_space=pltpu.SMEM), vmem, vmem, vmem],
        out_specs=vmem,
        scratch_shapes=[
            pltpu.VMEM((n, 2, depth // 2, 2 * HD), jnp.bfloat16),
            pltpu.VMEM((rows, width), jnp.float32),
            pltpu.VMEM((rows, 2 * width), jnp.float32),
            pltpu.SemaphoreType.DMA((n,)),
            pltpu.SemaphoreType.DMA((n,)),
            pltpu.SemaphoreType.DMA((n,)),
            pltpu.SemaphoreType.DMA((n,)),
        ],
        compiler_params=pltpu.CompilerParams(
            collective_id=0, has_side_effects=True, vmem_limit_bytes=48 << 20
        ),
    )(lengths, queries, suffix_kv.reshape(rows, 2 * HD), prompt_kv.reshape(depth, 2 * HD))


def solution(mesh):
    placed = (
        P(("groups", "loop"), ("heads", "pair")),
        P(("groups", "loop"), "heads", None),
        P(("groups", "loop"), "heads", None),
        P("groups"),
    )
    return jax.shard_map(
        shards,
        mesh=mesh,
        in_specs=placed,
        out_specs=P(("groups", "loop"), ("heads", "pair")),
        check_vma=False,
    )
```

```python
import functools
import math

import jax
import jax.numpy as jnp
from jax import lax
from jax.experimental import pallas as pl
from jax.experimental.pallas import tpu as pltpu
from jax.sharding import PartitionSpec as P

HD = 128
AG_DEV = 2
MAXLEN = 320
TILE = 128
SPAN = 256
NEG = -1e30
MESH = pl.DeviceIdType.MESH


def ones_beside(values):
    return jnp.concatenate([values, jnp.ones_like(values)], axis=1)


def scores_of(q, keys):
    return lax.dot_general(q, keys, (((1,), (1,)), ((), ())), preferred_element_type=jnp.float32)


def kernel(
    n, factor, len_hbm, q_hbm, sfx_hbm, prm_hbm, out_ref,
    held, q_ref, sfx_ref, len_ref, waiting, peak, best, acc, in_sem, send_sem, recv_sem, pass_sem, got_sem,
):
    rows, width = q_ref.shape
    heads = width // HD
    tiles = rows // TILE
    half = prm_hbm.shape[0] // 2
    me = lax.axis_index("loop")
    core = lax.axis_index("pair")
    barrier = pltpu.get_barrier_semaphore()

    def each_other(do):
        for d in range(1, n):
            for other in (me - d, me + d):

                @pl.when((other >= 0) & (other < n))
                def _(other=other):
                    do(other)

    each_other(
        lambda other: pl.semaphore_signal(barrier, inc=1, device_id={"loop": other}, device_id_type=MESH)
    )
    pl.semaphore_signal(barrier, inc=1, device_id={"pair": 1 - core}, device_id_type=MESH)

    fetches = [
        pltpu.make_async_copy(q_hbm, q_ref, in_sem.at[0]),
        pltpu.make_async_copy(sfx_hbm, sfx_ref, in_sem.at[1]),
        pltpu.make_async_copy(len_hbm, len_ref, in_sem.at[2]),
        pltpu.make_async_copy(prm_hbm.at[pl.ds(0, half), :], held.at[me, 0], in_sem.at[3]),
        pltpu.make_async_copy(prm_hbm.at[pl.ds(half, half), :], held.at[me, 1], in_sem.at[4]),
    ]
    for fetch in fetches:
        fetch.start()

    def clear(t, carry):
        part = pl.ds(pl.multiple_of(t * TILE, TILE), TILE)
        best[part, :] = jnp.full((TILE, HD), NEG, jnp.float32)
        acc[part, :] = jnp.zeros((TILE, 2 * HD), jnp.float32)
        return carry

    lax.fori_loop(0, tiles * heads, clear, 0)
    pl.semaphore_wait(barrier, n)

    def out_copy(other):
        return pltpu.make_async_remote_copy(
            src_ref=prm_hbm.at[pl.ds(pl.multiple_of(core * half, half), half), :],
            dst_ref=held.at[me, core],
            send_sem=send_sem.at[other],
            recv_sem=recv_sem.at[me],
            device_id={"loop": other},
            device_id_type=MESH,
        )

    each_other(lambda other: out_copy(other).start())

    def source(k):
        both = jnp.minimum(me, n - 1 - me)
        near = (k + 1) // 2
        paired = jnp.where(k % 2 == 1, me - near, me + near)
        far = k - both
        lone = jnp.where(me > n - 1 - me, me - far, me + far)
        return jnp.where(k == 0, me, jnp.where(k <= 2 * both, paired, lone))

    def arrived(src):
        pltpu.make_async_remote_copy(
            src_ref=held.at[src, core],
            dst_ref=held.at[src, core],
            send_sem=send_sem.at[src],
            recv_sem=recv_sem.at[src],
            device_id={"loop": src},
            device_id_type=MESH,
        ).wait_recv()

    def hand_over(src, which):
        return pltpu.make_async_remote_copy(
            src_ref=held.at[src, which],
            dst_ref=held.at[src, which],
            send_sem=pass_sem.at[src],
            recv_sem=got_sem.at[src],
            device_id={"pair": 1 - core},
            device_id_type=MESH,
        )

    def head_rows(at):
        return jnp.concatenate(
            [q_ref[pl.ds(at, TILE), pl.ds(h * HD, HD)] for h in range(heads)], axis=0
        )

    def score(at, keys, mask):
        s = scores_of(head_rows(at), keys)
        if mask is not None:
            s = jnp.where(jnp.concatenate([mask] * heads, axis=0), s, NEG)
        waiting[...] = s
        peak[...] = jnp.broadcast_to(jnp.max(s, axis=1, keepdims=True), peak.shape)

    def weigh(at, values):
        stack = pl.ds(pl.multiple_of(at * heads, TILE), heads * TILE)
        s = waiting[...]
        old = best[stack, :]
        top = jnp.maximum(old, peak[...])
        shrink = jnp.exp2((old - top) * factor)
        w = jnp.exp2((s - jnp.concatenate([top] * (s.shape[1] // HD), axis=1)) * factor)
        new = jnp.dot(w.astype(jnp.bfloat16), ones_beside(values), preferred_element_type=jnp.float32)
        best[stack, :] = top
        acc[stack, :] = acc[stack, :] * jnp.concatenate([shrink, shrink], axis=1) + new

    fetches[0].wait()
    fetches[1].wait()
    fetches[2].wait()
    first_end = len_ref[me * AG_DEV]
    live_end = first_end + len_ref[me * AG_DEV + 1]

    counts = [
        -(-min((t + 1) * TILE, TILE + MAXLEN - 1) // SPAN) for t in range(tiles)
    ]

    def suffix_item(i):
        t, j, begun = 0, i, 0
        for count in counts[:-1]:
            begun += count
            past = (i >= begun).astype(jnp.int32)
            t = t + past
            j = j - past * count
        at = pl.multiple_of(t * TILE, TILE)
        stop = at + TILE - j * SPAN
        return at, pl.multiple_of(jnp.maximum(stop - SPAN, 0), TILE), stop

    def suffix_score(i):
        at, low, stop = suffix_item(i)
        row_at = at + lax.broadcasted_iota(jnp.int32, (TILE, SPAN), 0)
        key_at = low + lax.broadcasted_iota(jnp.int32, (TILE, SPAN), 1)
        begin = jnp.where(row_at >= first_end, first_end, 0)
        mask = (key_at <= jnp.minimum(row_at, stop - 1)) & (key_at >= begin)
        score(at, sfx_ref[pl.ds(low, SPAN), :HD], mask)

    def suffix_step(i, carry):
        at, low, _ = suffix_item(i)
        weigh(at, sfx_ref[pl.ds(low, SPAN), HD:])
        suffix_score(jnp.minimum(i + 1, sum(counts) - 1))
        return carry

    suffix_score(jnp.int32(0))
    lax.fori_loop(0, sum(counts), suffix_step, 0)
    fetches[3].wait()
    fetches[4].wait()

    def prompt_score(i):
        at = pl.multiple_of(lax.rem(i, tiles) * TILE, TILE)
        score(at, held[source(i // tiles)].reshape(2 * half, 2 * HD)[:, :HD], None)

    def prompt_step(i, carry):
        k = i // tiles
        t = lax.rem(i, tiles)

        @pl.when((t == 0) & (k < n - 1))
        def _():
            following = source(k + 1)
            arrived(following)
            hand_over(following, core).start()

        @pl.when((t == tiles - 1) & (k < n - 1))
        def _():
            hand_over(source(k + 1), 1 - core).wait_recv()

        weigh(pl.multiple_of(t * TILE, TILE), held[source(k)].reshape(2 * half, 2 * HD)[:, HD:])
        prompt_score(jnp.minimum(i + 1, n * tiles - 1))
        return carry

    prompt_score(jnp.int32(0))
    lax.fori_loop(0, n * tiles, prompt_step, 0)

    def finish(t, carry):
        at = pl.multiple_of(t * TILE, TILE)
        live = at + lax.broadcasted_iota(jnp.int32, (TILE, HD), 0) < live_end
        for h in range(heads):
            part = pl.ds(pl.multiple_of(at * heads + h * TILE, TILE), TILE)
            result = jnp.where(live, acc[part, :HD] / acc[part, HD:], 0.0)
            out_ref[pl.ds(at, TILE), pl.ds(h * HD, HD)] = result.astype(out_ref.dtype)
        return carry

    lax.fori_loop(0, tiles, finish, 0)

    each_other(lambda other: out_copy(other).wait_send())
    each_other(lambda other: hand_over(other, core).wait_send())


def shards(queries, suffix_kv, prompt_kv, lengths):
    n = lax.axis_size("loop")
    rows, width = queries.shape
    heads = width // HD
    depth = prompt_kv.shape[0]
    factor = math.log2(math.e) / math.sqrt(HD)
    vmem = pl.BlockSpec(memory_space=pltpu.VMEM)
    return pl.pallas_call(
        functools.partial(kernel, n, factor),
        out_shape=jax.ShapeDtypeStruct((rows, width), jnp.bfloat16),
        in_specs=[pl.BlockSpec(memory_space=pltpu.HBM)] * 4,
        out_specs=vmem,
        scratch_shapes=[
            pltpu.VMEM((n, 2, depth // 2, 2 * HD), jnp.bfloat16),
            pltpu.VMEM((rows, width), jnp.bfloat16),
            pltpu.VMEM((rows, 2 * HD), jnp.bfloat16),
            pltpu.SMEM(lengths.shape, jnp.int32),
            pltpu.VMEM((TILE * heads, SPAN), jnp.float32),
            pltpu.VMEM((TILE * heads, HD), jnp.float32),
            pltpu.VMEM((rows * heads, HD), jnp.float32),
            pltpu.VMEM((rows * heads, 2 * HD), jnp.float32),
            pltpu.SemaphoreType.DMA((5,)),
            pltpu.SemaphoreType.DMA((n,)),
            pltpu.SemaphoreType.DMA((n,)),
            pltpu.SemaphoreType.DMA((n,)),
            pltpu.SemaphoreType.DMA((n,)),
        ],
        compiler_params=pltpu.CompilerParams(
            collective_id=0, has_side_effects=True, vmem_limit_bytes=56000 << 10
        ),
    )(lengths, queries, suffix_kv.reshape(rows, 2 * HD), prompt_kv.reshape(depth, 2 * HD))


def solution(mesh):
    placed = (
        P(("groups", "loop"), ("heads", "pair")),
        P(("groups", "loop"), "heads", None),
        P(("groups", "loop"), "heads", None),
        P("groups"),
    )
    return jax.shard_map(
        shards,
        mesh=mesh,
        in_specs=placed,
        out_specs=P(("groups", "loop"), ("heads", "pair")),
        check_vma=False,
    )
```

```python
import functools
import math

import jax
import jax.numpy as jnp
from jax import lax
from jax.experimental import pallas as pl
from jax.experimental.pallas import tpu as pltpu
from jax.sharding import PartitionSpec as P

HD = 128
AG_DEV = 2
MAXLEN = 320
TILE = 128
SPAN = 256
TOGETHER = 2
NEG = -1e30
MESH = pl.DeviceIdType.MESH


def ones_beside(values):
    return jnp.concatenate([values, jnp.ones_like(values)], axis=1)


def scores_of(q, keys):
    return lax.dot_general(q, keys, (((1,), (1,)), ((), ())), preferred_element_type=jnp.float32)


def kernel(
    n, factor, len_hbm, q_hbm, sfx_hbm, prm_hbm, out_ref,
    held, q_ref, sfx_ref, len_ref, waiting, peak, best, acc, in_sem, send_sem, recv_sem, pass_sem, got_sem,
):
    rows, width = q_ref.shape
    heads = width // HD
    tiles = rows // TILE
    half = prm_hbm.shape[0] // 2
    together = TOGETHER if heads % TOGETHER == 0 else 1
    me = lax.axis_index("loop")
    core = lax.axis_index("pair")
    barrier = pltpu.get_barrier_semaphore()

    def each_other(do):
        for d in range(1, n):
            for other in (me - d, me + d):

                @pl.when((other >= 0) & (other < n))
                def _(other=other):
                    do(other)

    each_other(
        lambda other: pl.semaphore_signal(barrier, inc=1, device_id={"loop": other}, device_id_type=MESH)
    )
    pl.semaphore_signal(barrier, inc=1, device_id={"pair": 1 - core}, device_id_type=MESH)

    fetches = [
        pltpu.make_async_copy(q_hbm, q_ref, in_sem.at[0]),
        pltpu.make_async_copy(sfx_hbm, sfx_ref, in_sem.at[1]),
        pltpu.make_async_copy(len_hbm, len_ref, in_sem.at[2]),
        pltpu.make_async_copy(prm_hbm.at[pl.ds(0, half), :], held.at[me, 0], in_sem.at[3]),
        pltpu.make_async_copy(prm_hbm.at[pl.ds(half, half), :], held.at[me, 1], in_sem.at[4]),
    ]
    for fetch in fetches:
        fetch.start()

    def clear(t, carry):
        part = pl.ds(pl.multiple_of(t * TILE, TILE), TILE)
        best[part, :] = jnp.full((TILE, HD), NEG, jnp.float32)
        acc[part, :] = jnp.zeros((TILE, 2 * HD), jnp.float32)
        return carry

    lax.fori_loop(0, tiles * heads, clear, 0)
    pl.semaphore_wait(barrier, n)

    def out_copy(other):
        return pltpu.make_async_remote_copy(
            src_ref=prm_hbm.at[pl.ds(pl.multiple_of(core * half, half), half), :],
            dst_ref=held.at[me, core],
            send_sem=send_sem.at[other],
            recv_sem=recv_sem.at[me],
            device_id={"loop": other},
            device_id_type=MESH,
        )

    each_other(lambda other: out_copy(other).start())

    def source(k):
        both = jnp.minimum(me, n - 1 - me)
        near = (k + 1) // 2
        paired = jnp.where(k % 2 == 1, me - near, me + near)
        far = k - both
        lone = jnp.where(me > n - 1 - me, me - far, me + far)
        return jnp.where(k == 0, me, jnp.where(k <= 2 * both, paired, lone))

    def arrived(src):
        pltpu.make_async_remote_copy(
            src_ref=held.at[src, core],
            dst_ref=held.at[src, core],
            send_sem=send_sem.at[src],
            recv_sem=recv_sem.at[src],
            device_id={"loop": src},
            device_id_type=MESH,
        ).wait_recv()

    def hand_over(src, which):
        return pltpu.make_async_remote_copy(
            src_ref=held.at[src, which],
            dst_ref=held.at[src, which],
            send_sem=pass_sem.at[src],
            recv_sem=got_sem.at[src],
            device_id={"pair": 1 - core},
            device_id_type=MESH,
        )

    def score(at, keys, mask, g):
        q = jnp.concatenate(
            [q_ref[pl.ds(at, TILE), pl.ds(h * HD, HD)] for h in range(g * together, (g + 1) * together)],
            axis=0,
        )
        s = scores_of(q, keys)
        if mask is not None:
            s = jnp.where(jnp.concatenate([mask] * together, axis=0), s, NEG)
        return s

    def keep(s, g):
        part = pl.ds(g * together * TILE, together * TILE)
        waiting[part, :] = s
        peak[part, :] = jnp.broadcast_to(jnp.max(s, axis=1, keepdims=True), (together * TILE, HD))

    def weigh(at, values, g):
        part = pl.ds(g * together * TILE, together * TILE)
        stack = pl.ds(pl.multiple_of(at * heads + g * together * TILE, TILE), together * TILE)
        s = waiting[part, :]
        old = best[stack, :]
        top = jnp.maximum(old, peak[part, :])
        shrink = jnp.exp2((old - top) * factor)
        w = jnp.exp2((s - jnp.concatenate([top] * (s.shape[1] // HD), axis=1)) * factor)
        new = jnp.dot(w.astype(jnp.bfloat16), values, preferred_element_type=jnp.float32)
        best[stack, :] = top
        acc[stack, :] = acc[stack, :] * jnp.concatenate([shrink, shrink], axis=1) + new

    def advance(at, values, at_next, keys_next, mask_next):
        values = ones_beside(values)
        for g in range(heads // together):
            weigh(at, values, g)
            keep(score(at_next, keys_next, mask_next, g), g)

    def begin_with(at, keys, mask):
        for g in range(heads // together):
            keep(score(at, keys, mask, g), g)

    fetches[0].wait()
    fetches[1].wait()
    fetches[2].wait()
    first_end = len_ref[me * AG_DEV]
    live_end = first_end + len_ref[me * AG_DEV + 1]

    counts = [
        -(-min((t + 1) * TILE, TILE + MAXLEN - 1) // SPAN) for t in range(tiles)
    ]

    def suffix_item(i):
        t, j, begun = 0, i, 0
        for count in counts[:-1]:
            begun += count
            past = (i >= begun).astype(jnp.int32)
            t = t + past
            j = j - past * count
        at = pl.multiple_of(t * TILE, TILE)
        stop = at + TILE - j * SPAN
        return at, pl.multiple_of(jnp.maximum(stop - SPAN, 0), TILE), stop

    def suffix_operands(i):
        at, low, stop = suffix_item(i)
        row_at = at + lax.broadcasted_iota(jnp.int32, (TILE, SPAN), 0)
        key_at = low + lax.broadcasted_iota(jnp.int32, (TILE, SPAN), 1)
        begin = jnp.where(row_at >= first_end, first_end, 0)
        mask = (key_at <= jnp.minimum(row_at, stop - 1)) & (key_at >= begin)
        return at, sfx_ref[pl.ds(low, SPAN), :HD], mask

    def suffix_step(i, carry):
        at, low, _ = suffix_item(i)
        advance(at, sfx_ref[pl.ds(low, SPAN), HD:], *suffix_operands(jnp.minimum(i + 1, sum(counts) - 1)))
        return carry

    begin_with(*suffix_operands(jnp.int32(0)))
    lax.fori_loop(0, sum(counts), suffix_step, 0)
    fetches[3].wait()
    fetches[4].wait()

    def tile_of(t, src):
        at = pl.multiple_of(t * TILE, TILE)
        return at, held[src].reshape(2 * half, 2 * HD)[:, :HD], None

    def prompt_shard(k, src):
        following = source(jnp.minimum(k + 1, n - 1))

        @pl.when(k < n - 1)
        def _():
            arrived(following)
            hand_over(following, core).start()

        def prompt_tile(t, carry):
            turn = t == tiles - 1

            @pl.when(turn & (k < n - 1))
            def _():
                hand_over(following, 1 - core).wait_recv()

            values = held[src].reshape(2 * half, 2 * HD)[:, HD:]
            ahead = tile_of(jnp.where(turn, 0, t + 1), jnp.where(turn, following, src))
            advance(pl.multiple_of(t * TILE, TILE), values, *ahead)
            return carry

        lax.fori_loop(0, tiles, prompt_tile, 0)
        return following

    begin_with(*tile_of(0, me))
    lax.fori_loop(0, n, prompt_shard, me)

    def finish(t, carry):
        at = pl.multiple_of(t * TILE, TILE)
        live = at + lax.broadcasted_iota(jnp.int32, (TILE, HD), 0) < live_end
        for h in range(heads):
            part = pl.ds(pl.multiple_of(at * heads + h * TILE, TILE), TILE)
            result = jnp.where(live, acc[part, :HD] / acc[part, HD:], 0.0)
            out_ref[pl.ds(at, TILE), pl.ds(h * HD, HD)] = result.astype(out_ref.dtype)
        return carry

    lax.fori_loop(0, tiles, finish, 0)

    each_other(lambda other: out_copy(other).wait_send())
    each_other(lambda other: hand_over(other, core).wait_send())


def shards(queries, suffix_kv, prompt_kv, lengths):
    n = lax.axis_size("loop")
    rows, width = queries.shape
    heads = width // HD
    depth = prompt_kv.shape[0]
    factor = math.log2(math.e) / math.sqrt(HD)
    vmem = pl.BlockSpec(memory_space=pltpu.VMEM)
    attended = pl.pallas_call(
        functools.partial(kernel, n, factor),
        out_shape=jax.ShapeDtypeStruct((rows, width), jnp.bfloat16),
        in_specs=[pl.BlockSpec(memory_space=pltpu.HBM)] * 4,
        out_specs=vmem,
        scratch_shapes=[
            pltpu.VMEM((n, 2, depth // 2, 2 * HD), jnp.bfloat16),
            pltpu.VMEM((rows, width), jnp.bfloat16),
            pltpu.VMEM((rows, 2 * HD), jnp.bfloat16),
            pltpu.SMEM(lengths.shape, jnp.int32),
            pltpu.VMEM((TILE * heads, SPAN), jnp.float32),
            pltpu.VMEM((TILE * heads, HD), jnp.float32),
            pltpu.VMEM((rows * heads, HD), jnp.float32),
            pltpu.VMEM((rows * heads, 2 * HD), jnp.float32),
            pltpu.SemaphoreType.DMA((5,)),
            pltpu.SemaphoreType.DMA((n,)),
            pltpu.SemaphoreType.DMA((n,)),
            pltpu.SemaphoreType.DMA((n,)),
            pltpu.SemaphoreType.DMA((n,)),
        ],
        compiler_params=pltpu.CompilerParams(
            collective_id=0, has_side_effects=True, vmem_limit_bytes=56000 << 10
        ),
    )(lengths, queries, suffix_kv.reshape(rows, 2 * HD), prompt_kv.reshape(depth, 2 * HD))
    nothing = jnp.minimum(lax.axis_index("loop"), 0).astype(attended.dtype)
    return attended + nothing


def solution(mesh):
    placed = (
        P(("groups", "loop"), ("heads", "pair")),
        P(("groups", "loop"), "heads", None),
        P(("groups", "loop"), "heads", None),
        P("groups"),
    )
    return jax.shard_map(
        shards,
        mesh=mesh,
        in_specs=placed,
        out_specs=P(("groups", "loop"), ("heads", "pair")),
        check_vma=False,
    )
```

```python
import functools
import math

import jax
import jax.numpy as jnp
from jax import lax
from jax.experimental import pallas as pl
from jax.experimental.pallas import tpu as pltpu
from jax.sharding import PartitionSpec as P

HD = 128
AG_DEV = 2
MAXLEN = 320
TILE = 320
SPAN = 256
TOGETHER = 2
NEG = -1e30
MESH = pl.DeviceIdType.MESH


def ones_beside(values):
    return jnp.concatenate([values, jnp.ones_like(values)], axis=1)


def scores_of(q, keys):
    return lax.dot_general(q, keys, (((1,), (1,)), ((), ())), preferred_element_type=jnp.float32)


def kernel(
    n, factor, len_hbm, q_hbm, sfx_hbm, prm_hbm, out_ref,
    held, q_ref, sfx_ref, len_ref, waiting, peak, best, acc, in_sem, send_sem, recv_sem, pass_sem, got_sem,
):
    rows, width = q_ref.shape
    heads = width // HD
    tiles = rows // TILE
    half = prm_hbm.shape[0] // 2
    together = TOGETHER if heads % TOGETHER == 0 else 1
    me = lax.axis_index("loop")
    core = lax.axis_index("pair")
    barrier = pltpu.get_barrier_semaphore()

    def each_other(do):
        for d in range(1, n):
            for other in (me - d, me + d):

                @pl.when((other >= 0) & (other < n))
                def _(other=other):
                    do(other)

    each_other(
        lambda other: pl.semaphore_signal(barrier, inc=1, device_id={"loop": other}, device_id_type=MESH)
    )
    pl.semaphore_signal(barrier, inc=1, device_id={"pair": 1 - core}, device_id_type=MESH)

    fetches = [
        pltpu.make_async_copy(q_hbm, q_ref, in_sem.at[0]),
        pltpu.make_async_copy(sfx_hbm, sfx_ref, in_sem.at[1]),
        pltpu.make_async_copy(len_hbm, len_ref, in_sem.at[2]),
        pltpu.make_async_copy(prm_hbm.at[pl.ds(0, half), :], held.at[me, 0], in_sem.at[3]),
        pltpu.make_async_copy(prm_hbm.at[pl.ds(half, half), :], held.at[me, 1], in_sem.at[4]),
    ]
    for fetch in fetches:
        fetch.start()

    def clear(t, carry):
        part = pl.ds(pl.multiple_of(t * TILE, TILE), TILE)
        best[part, :] = jnp.full((TILE, HD), NEG, jnp.float32)
        acc[part, :] = jnp.zeros((TILE, 2 * HD), jnp.float32)
        return carry

    lax.fori_loop(0, tiles * heads, clear, 0)
    pl.semaphore_wait(barrier, n)

    def out_copy(other):
        return pltpu.make_async_remote_copy(
            src_ref=prm_hbm.at[pl.ds(pl.multiple_of(core * half, half), half), :],
            dst_ref=held.at[me, core],
            send_sem=send_sem.at[other],
            recv_sem=recv_sem.at[me],
            device_id={"loop": other},
            device_id_type=MESH,
        )

    each_other(lambda other: out_copy(other).start())

    def source(k):
        both = jnp.minimum(me, n - 1 - me)
        near = (k + 1) // 2
        paired = jnp.where(k % 2 == 1, me - near, me + near)
        far = k - both
        lone = jnp.where(me > n - 1 - me, me - far, me + far)
        return jnp.where(k == 0, me, jnp.where(k <= 2 * both, paired, lone))

    def arrived(src):
        pltpu.make_async_remote_copy(
            src_ref=held.at[src, core],
            dst_ref=held.at[src, core],
            send_sem=send_sem.at[src],
            recv_sem=recv_sem.at[src],
            device_id={"loop": src},
            device_id_type=MESH,
        ).wait_recv()

    def hand_over(src, which):
        return pltpu.make_async_remote_copy(
            src_ref=held.at[src, which],
            dst_ref=held.at[src, which],
            send_sem=pass_sem.at[src],
            recv_sem=got_sem.at[src],
            device_id={"pair": 1 - core},
            device_id_type=MESH,
        )

    def score(at, keys, mask, g):
        q = jnp.concatenate(
            [q_ref[pl.ds(at, TILE), pl.ds(h * HD, HD)] for h in range(g * together, (g + 1) * together)],
            axis=0,
        )
        s = scores_of(q, keys)
        if mask is not None:
            s = jnp.where(jnp.concatenate([mask] * together, axis=0), s, NEG)
        return s

    def keep(s, g):
        part = pl.ds(g * together * TILE, together * TILE)
        waiting[part, :] = s
        peak[part, :] = jnp.broadcast_to(jnp.max(s, axis=1, keepdims=True), (together * TILE, HD))

    def weigh(at, values, g):
        part = pl.ds(g * together * TILE, together * TILE)
        stack = pl.ds(pl.multiple_of(at * heads + g * together * TILE, TILE), together * TILE)
        s = waiting[part, :]
        old = best[stack, :]
        top = jnp.maximum(old, peak[part, :])
        shrink = jnp.exp2((old - top) * factor)
        w = jnp.exp2((s - jnp.concatenate([top] * (s.shape[1] // HD), axis=1)) * factor)
        new = jnp.dot(w.astype(jnp.bfloat16), values, preferred_element_type=jnp.float32)
        best[stack, :] = top
        acc[stack, :] = acc[stack, :] * jnp.concatenate([shrink, shrink], axis=1) + new

    def advance(at, values, at_next, keys_next, mask_next):
        values = ones_beside(values)
        for g in range(heads // together):
            weigh(at, values, g)
            keep(score(at_next, keys_next, mask_next, g), g)

    def begin_with(at, keys, mask):
        for g in range(heads // together):
            keep(score(at, keys, mask, g), g)

    fetches[0].wait()
    fetches[1].wait()
    fetches[2].wait()
    first_end = len_ref[me * AG_DEV]
    live_end = first_end + len_ref[me * AG_DEV + 1]

    counts = [
        -(-min((t + 1) * TILE, TILE + MAXLEN - 1) // SPAN) for t in range(tiles)
    ]

    def suffix_item(i):
        t, j, begun = 0, i, 0
        for count in counts[:-1]:
            begun += count
            past = (i >= begun).astype(jnp.int32)
            t = t + past
            j = j - past * count
        at = pl.multiple_of(t * TILE, TILE)
        stop = at + TILE - j * SPAN
        return at, pl.multiple_of(jnp.maximum(stop - SPAN, 0), math.gcd(TILE, SPAN)), stop

    def suffix_operands(i):
        at, low, stop = suffix_item(i)
        row_at = at + lax.broadcasted_iota(jnp.int32, (TILE, SPAN), 0)
        key_at = low + lax.broadcasted_iota(jnp.int32, (TILE, SPAN), 1)
        begin = jnp.where(row_at >= first_end, first_end, 0)
        mask = (key_at <= jnp.minimum(row_at, stop - 1)) & (key_at >= begin)
        return at, sfx_ref[pl.ds(low, SPAN), :HD], mask

    def suffix_step(i, carry):
        at, low, _ = suffix_item(i)
        advance(at, sfx_ref[pl.ds(low, SPAN), HD:], *suffix_operands(jnp.minimum(i + 1, sum(counts) - 1)))
        return carry

    begin_with(*suffix_operands(jnp.int32(0)))
    lax.fori_loop(0, sum(counts), suffix_step, 0)
    fetches[3].wait()
    fetches[4].wait()

    def tile_of(t, src):
        at = pl.multiple_of(t * TILE, TILE)
        return at, held[src].reshape(2 * half, 2 * HD)[:, :HD], None

    def prompt_shard(k, src):
        following = source(jnp.minimum(k + 1, n - 1))

        @pl.when(k < n - 1)
        def _():
            arrived(following)
            hand_over(following, core).start()

        def prompt_tile(t, carry):
            turn = t == tiles - 1

            @pl.when(turn & (k < n - 1))
            def _():
                hand_over(following, 1 - core).wait_recv()

            values = held[src].reshape(2 * half, 2 * HD)[:, HD:]
            ahead = tile_of(jnp.where(turn, 0, t + 1), jnp.where(turn, following, src))
            advance(pl.multiple_of(t * TILE, TILE), values, *ahead)
            return carry

        lax.fori_loop(0, tiles, prompt_tile, 0)
        return following

    begin_with(*tile_of(0, me))
    lax.fori_loop(0, n, prompt_shard, me)

    def finish(t, carry):
        at = pl.multiple_of(t * TILE, TILE)
        live = at + lax.broadcasted_iota(jnp.int32, (TILE, HD), 0) < live_end
        for h in range(heads):
            part = pl.ds(pl.multiple_of(at * heads + h * TILE, TILE), TILE)
            result = jnp.where(live, acc[part, :HD] / acc[part, HD:], 0.0)
            out_ref[pl.ds(at, TILE), pl.ds(h * HD, HD)] = result.astype(out_ref.dtype)
        return carry

    lax.fori_loop(0, tiles, finish, 0)

    each_other(lambda other: out_copy(other).wait_send())
    each_other(lambda other: hand_over(other, core).wait_send())


def shards(queries, suffix_kv, prompt_kv, lengths):
    n = lax.axis_size("loop")
    rows, width = queries.shape
    heads = width // HD
    depth = prompt_kv.shape[0]
    factor = math.log2(math.e) / math.sqrt(HD)
    vmem = pl.BlockSpec(memory_space=pltpu.VMEM)
    attended = pl.pallas_call(
        functools.partial(kernel, n, factor),
        out_shape=jax.ShapeDtypeStruct((rows, width), jnp.bfloat16),
        in_specs=[pl.BlockSpec(memory_space=pltpu.HBM)] * 4,
        out_specs=vmem,
        scratch_shapes=[
            pltpu.VMEM((n, 2, depth // 2, 2 * HD), jnp.bfloat16),
            pltpu.VMEM((rows, width), jnp.bfloat16),
            pltpu.VMEM((rows, 2 * HD), jnp.bfloat16),
            pltpu.SMEM(lengths.shape, jnp.int32),
            pltpu.VMEM((TILE * heads, SPAN), jnp.float32),
            pltpu.VMEM((TILE * heads, HD), jnp.float32),
            pltpu.VMEM((rows * heads, HD), jnp.float32),
            pltpu.VMEM((rows * heads, 2 * HD), jnp.float32),
            pltpu.SemaphoreType.DMA((5,)),
            pltpu.SemaphoreType.DMA((n,)),
            pltpu.SemaphoreType.DMA((n,)),
            pltpu.SemaphoreType.DMA((n,)),
            pltpu.SemaphoreType.DMA((n,)),
        ],
        compiler_params=pltpu.CompilerParams(
            collective_id=0, has_side_effects=True, vmem_limit_bytes=56000 << 10
        ),
    )(lengths, queries, suffix_kv.reshape(rows, 2 * HD), prompt_kv.reshape(depth, 2 * HD))
    nothing = jnp.minimum(lax.axis_index("loop"), 0).astype(attended.dtype)
    return attended + nothing


def solution(mesh):
    placed = (
        P(("groups", "loop"), ("heads", "pair")),
        P(("groups", "loop"), "heads", None),
        P(("groups", "loop"), "heads", None),
        P("groups"),
    )
    return jax.shard_map(
        shards,
        mesh=mesh,
        in_specs=placed,
        out_specs=P(("groups", "loop"), ("heads", "pair")),
        check_vma=False,
    )
```
